32 devices in a mesh: ia: 4 (over x, core), ja: 2 (over y), ka: 4 (over z).
Axes of the slice: x: 2, y: 2, z: 4, core: 2. Of those that a mesh axis runs over, the one named last changes fastest.
Arguments:
- tensor: float32 [128, 256, 512], P('ia', 'ja', 'ka'), may hold values from -200 to 200
- factor_b: float32 [256, 4, 96], P(('ja', 'ka')), may hold values from -4 to 4
- factor_c: float32 [512, 4, 96], P(('ka', 'ja')), may hold values from -4 to 4
Outputs:
- factor_a: float32 [128, 4, 96], P(('ia', 'ja', 'ka'))
- weights: float32 [4, 96], replicated
The draws below stay inside these ranges and needn't reach their ends.
All inputs are finite; a program needn't handle non-finite values.
Results may differ from the reference program's by a relative error of at most 0.0003.
Values sent between devices are 32-bit elements; how exact they have to be, the bound alone decides.
A program may use at most 64 MiB of HBM per device.

```python
import math
import jax
import jax.numpy as jnp
from jax import lax

R = 96
STARTS = 4
I = 128
J = 256
K = 512


def rising(key, count, top):
    places = jnp.arange(count, dtype=jnp.float32) / max(count - 1, 1)
    rough = jax.random.uniform(key, (count,), jnp.float32, 0.7, 1.4)
    return jnp.exp(places * math.log(top)) * rough


def factor_draw(key, count):
    keys = jax.random.split(key, 3)
    base = jax.random.truncated_normal(keys[0], -4.0, 4.0, (count, STARTS, R), jnp.float32)
    top_scale = 10.0
    row_scale = rising(keys[1], count, top_scale)
    col_scale = jnp.exp(jax.random.uniform(keys[2], (STARTS, R), jnp.float32, math.log(0.5), math.log(2.0)))
    return base * row_scale[:, None, None] * col_scale[None] * (0.2157 / math.sqrt(count))


def draw_tensor(key, part):
    keys = jax.random.split(key, 4)
    base = jax.random.truncated_normal(keys[0], -4.0, 4.0, (I, J, K), jnp.float32)
    top_scale = 10.0
    first = rising(keys[1], I, top_scale)
    second = rising(keys[2], J, 3.0)
    third = rising(keys[3], K, 3.0)
    return 0.2 * base * first[:, None, None] * second[None, :, None] * third[None, None, :]


def draw_factor_b(key, part):
    return factor_draw(jax.random.fold_in(key, 11), J)


def draw_factor_c(key, part):
    return factor_draw(jax.random.fold_in(key, 23), K)


def setup_inputs(seed: int = 0) -> dict:
    seeds = jax.random.split(jax.random.key(seed), 4)
    return {
        "tensor": draw_tensor(jax.random.fold_in(seeds[3], 71), 0),
        "factor_b": draw_factor_b(jax.random.fold_in(seeds[3], 71), 0),
        "factor_c": draw_factor_c(jax.random.fold_in(seeds[3], 71), 0),
    }


highest = lax.Precision.HIGHEST

def gram_of(rows):
    return jnp.einsum('jsr,jsq->srq', rows.astype(jnp.float32), rows.astype(jnp.float32), precision=highest, preferred_element_type=jnp.float32)

def solve_normal(rows, gram_b, gram_c):
    columns = []
    for member in range(rows.shape[1]):
        normal_mat = gram_b[member] * gram_c[member]
        factor_l = jnp.linalg.cholesky(normal_mat)
        right_side = rows[:, member, :].T
        lower_sol = lax.linalg.triangular_solve(factor_l, right_side, left_side=True, lower=True)
        upper_sol = lax.linalg.triangular_solve(factor_l, lower_sol, left_side=True, lower=True, transpose_a=True)
        columns.append(upper_sol.T)
    return jnp.stack(columns, axis=1)

def reference(tensor, factor_b, factor_c):
    rows_i, rows_j, rows_k = tensor.shape
    starts, col_count = (factor_b.shape[1], factor_b.shape[2])
    width = starts * col_count
    partial_value = jnp.dot(tensor.reshape(rows_i * rows_j, rows_k).astype(jnp.float32), factor_c.reshape(rows_k, width).astype(jnp.float32), precision=highest, preferred_element_type=jnp.float32).reshape(rows_i, rows_j, width)
    mttkrp = jnp.einsum('ijr,jr->ir', partial_value.astype(jnp.float32), factor_b.reshape(rows_j, width).astype(jnp.float32), precision=highest, preferred_element_type=jnp.float32)
    mttkrp = mttkrp.reshape(rows_i, starts, col_count)
    factor_raw = solve_normal(mttkrp, gram_of(factor_b), gram_of(factor_c))
    squares = lax.optimization_barrier(jnp.sum(factor_raw * factor_raw, axis=0))
    weights = jnp.sqrt(squares / rows_i + 1e-06)
    return (factor_raw / weights[None], weights)
```

```python
import functools

import jax
import jax.numpy as jnp
from jax import lax
from jax.experimental import pallas as pl
from jax.experimental.pallas import tpu as pltpu
from jax.sharding import PartitionSpec as P

MESH = pl.DeviceIdType.MESH
LANES = 128
SUBS = 8
HIGHEST = lax.Precision.HIGHEST


def solver_places(sizes, starts):
    na, nj, nk = sizes
    places = []
    for s in range(starts):
        ia = (s % 2) * (na // 2)
        ja = ((s // 2) * (nj // 2)) % nj
        ka = min(nk - 1, max(0, nk // 2 - 1 + (s // 2) % 2))
        places.append((ia, ja, ka))
    assert len(set(places)) == starts
    return places


def negative_inverse(tiles, cols):
    lane = lax.broadcasted_iota(jnp.int32, (SUBS, LANES), 1)
    sub = lax.broadcasted_iota(jnp.int32, (SUBS, LANES), 0)
    for k in range(0, cols, 2):
        v, p = k // SUBS, k % SUBS
        at0, at1 = lane == k, lane == k + 1
        both = at0 | at1
        row0 = jnp.broadcast_to(tiles[v][p : p + 1, :], (SUBS, LANES))
        row1 = jnp.broadcast_to(tiles[v][p + 1 : p + 2, :], (SUBS, LANES))
        col0 = [jnp.broadcast_to(t[:, k : k + 1], (SUBS, LANES)) for t in tiles]
        col1 = [jnp.broadcast_to(t[:, k + 1 : k + 2], (SUBS, LANES)) for t in tiles]
        a = jnp.broadcast_to(row0[:, k : k + 1], (SUBS, LANES))
        b = jnp.broadcast_to(row0[:, k + 1 : k + 2], (SUBS, LANES))
        d = jnp.broadcast_to(row1[:, k + 1 : k + 2], (SUBS, LANES))
        inv_a = 1.0 / a
        t = b * inv_a
        inv_s = 1.0 / (d - b * t)
        row0 = jnp.where(at0, -1.0, jnp.where(at1, 0.0, row0))
        row1 = jnp.where(at1, -1.0, jnp.where(at0, 0.0, row1))
        new1 = (row1 - t * row0) * inv_s
        new0 = row0 * inv_a - t * new1
        out = []
        for i, tile in enumerate(tiles):
            new = jnp.where(both, 0.0, tile) - col0[i] * new0 - col1[i] * new1
            if i == v:
                new = jnp.where(sub == p, new0, jnp.where(sub == p + 1, new1, new))
            out.append(new)
        tiles = out
    return tiles


def split(x):
    hi = x.astype(jnp.bfloat16)
    return hi, (x - hi.astype(jnp.float32)).astype(jnp.bfloat16)


def kernel(sizes, places, total_rows, t_ref, b_ref, c_ref, out_ref, w_ref,
           bg, cg, gb, gc, mp, mr, ob, orx,
           bs, br, cs, cr, gs, gbr, gcr, ms, mrs, os, ors):
    na, nj, nk = sizes
    group = nj * nk
    n = na * group
    starts, cols = b_ref.shape[1], b_ref.shape[2]
    rows_i = t_ref.shape[0]
    own_rows = out_ref.shape[0]
    ia, ja, ka = (lax.axis_index("ia"), lax.axis_index("ja"), lax.axis_index("ka"))
    g = ja * nk + ka
    me = ia * group + g
    ids = [(pa * nj + pj) * nk + pk for pa, pj, pk in places]

    def coords(d):
        return (d // group, (d // nk) % nj, d % nk)

    barrier = pltpu.get_barrier_semaphore()

    def greet(target):
        pl.semaphore_signal(barrier, inc=1, device_id=target, device_id_type=MESH)

    for o in range(1, nk):
        greet((ia, ja, lax.rem(ka + o, nk)))
    for o in range(1, nj):
        greet((ia, lax.rem(ja + o, nj), ka))
    for s, place in enumerate(places):
        @pl.when(me != ids[s])
        def _():
            greet(place)

        @pl.when(me == ids[s])
        def _():
            @pl.loop(1, n)
            def _(o):
                greet(coords(lax.rem(me + o, n)))

    for s in range(starts):
        bg[ka, s] = jnp.zeros(bg.shape[2:], jnp.float32)
        cg[ja, s] = jnp.zeros(cg.shape[2:], jnp.float32)
        bg[ka, s, :, 0:cols] = b_ref[:, s, :]
        cg[ja, s, :, 0:cols] = c_ref[:, s, :]

    is_solver = functools.reduce(jnp.logical_or, [me == d for d in ids])
    near = (nk - 1) + (nj - 1)

    @pl.when(is_solver)
    def _():
        pl.semaphore_wait(barrier, near + starts - 1 + n - 1)

    @pl.when(jnp.logical_not(is_solver))
    def _():
        pl.semaphore_wait(barrier, near + starts)

    def push(src, dst, send, recv, place, target_id, act):
        @pl.when(me == target_id)
        def _():
            if act == "start":
                pltpu.make_async_copy(src, dst, recv).start()

        @pl.when(me != target_id)
        def _():
            copy = pltpu.make_async_remote_copy(
                src_ref=src, dst_ref=dst, send_sem=send, recv_sem=recv,
                device_id=place, device_id_type=MESH)
            if act == "start":
                copy.start()
            else:
                copy.wait_send()

    def gram_rows(act):
        for s, place in enumerate(places):
            @pl.when(ia == place[0])
            def _():
                push(bg.at[ka, s], gb.at[g], gs.at[s], gbr, place, ids[s], act)

            @pl.when(ia == place[0] + 1)
            def _():
                push(cg.at[ja, s], gc.at[g], gs.at[s], gcr, place, ids[s], act)

    gram_rows("start")
    c_copies = []
    for o in range(1, nj):
        c_copies.append(pltpu.make_async_remote_copy(
            src_ref=cg.at[ja], dst_ref=cg.at[ja], send_sem=cs.at[o - 1], recv_sem=cr.at[o - 1],
            device_id=(ia, lax.rem(ja + o, nj), ka), device_id_type=MESH))
    b_copies = []
    for o in range(1, nk):
        b_copies.append(pltpu.make_async_remote_copy(
            src_ref=bg.at[ka], dst_ref=bg.at[ka], send_sem=bs.at[o - 1], recv_sem=br.at[o - 1],
            device_id=(ia, ja, lax.rem(ka + o, nk)), device_id_type=MESH))
    for copy in c_copies + b_copies:
        copy.start()
    for o in range(1, nj):
        src = cg.at[lax.rem(ja - o + nj, nj)]
        pltpu.make_async_copy(src, src, cr.at[o - 1]).wait()
    for o in range(1, nk):
        src = bg.at[lax.rem(ka - o + nk, nk)]
        pltpu.make_async_copy(src, src, br.at[o - 1]).wait()

    c_all = [jnp.concatenate([cg[q, s] for q in range(nj)], axis=0) for s in range(starts)]
    c_hi, c_lo = split(jnp.concatenate(c_all, axis=1))
    c_twice = jnp.concatenate([c_hi, c_hi], axis=0)
    b_all = jnp.concatenate(
        [jnp.concatenate([bg[q, s] for q in range(nk)], axis=0) for s in range(starts)], axis=1)
    rows_j, rows_k = t_ref.shape[1], t_ref.shape[2]
    step = SUBS

    @pl.loop(0, rows_i // step)
    def _(block):
        at = pl.multiple_of(block * step, step)
        t_hi, t_lo = split(t_ref[pl.ds(at, step)].reshape(step * rows_j, rows_k))
        part = jnp.dot(jnp.concatenate([t_hi, t_lo], axis=1), c_twice,
                       preferred_element_type=jnp.float32)
        part = part + jnp.dot(t_hi, c_lo, preferred_element_type=jnp.float32)
        summed = jnp.sum(part.reshape(step, rows_j, starts * LANES) * b_all[None], axis=1)
        for s in range(starts):
            mp[s, pl.ds(at, step), :] = summed[:, s * LANES : (s + 1) * LANES]

    def mttkrp_rows(act):
        for s, place in enumerate(places):
            push(mp.at[s], mr.at[me], ms.at[s], mrs, place, ids[s], act)

    mttkrp_rows("start")

    @pl.when(is_solver)
    def _():
        pltpu.make_async_copy(gb, gb, gbr).wait()
        pltpu.make_async_copy(gc, gc, gcr).wait()
        over_rows = (((0,), (0,)), ((), ()))
        rows_b = gb[...].reshape(gb.shape[0] * gb.shape[1], LANES)
        rows_c = gc[...].reshape(gc.shape[0] * gc.shape[1], LANES)
        gram_b = lax.dot_general(rows_b, rows_b, over_rows, precision=HIGHEST,
                                 preferred_element_type=jnp.float32)
        gram_c = lax.dot_general(rows_c, rows_c, over_rows, precision=HIGHEST,
                                 preferred_element_type=jnp.float32)
        normal = gram_b * gram_c
        tiles = [normal[i : i + SUBS, :] for i in range(0, cols, SUBS)]
        tiles = negative_inverse(tiles, cols)
        minus = jnp.concatenate(
            tiles + [jnp.zeros((LANES - cols, LANES), jnp.float32)], axis=0)

        pltpu.make_async_copy(mr, mr, mrs).wait()
        blocks = []
        for q in range(na):
            blocks.append(lax.fori_loop(
                1, group, lambda h, acc, q=q: acc + mr[q * group + h], mr[q * group]))
        mttkrp = jnp.concatenate(blocks, axis=0)
        raw = -jnp.dot(mttkrp, minus, precision=HIGHEST, preferred_element_type=jnp.float32)
        weight = jnp.sqrt(jnp.sum(raw * raw, axis=0, keepdims=True) / total_rows + 1e-06)
        final = raw / weight
        for d in range(n):
            ob[d, 0:own_rows, :] = final[d * own_rows : (d + 1) * own_rows, :]
            ob[d, own_rows : own_rows + 1, :] = weight

        for s in range(starts):
            @pl.when(me == ids[s])
            def _():
                pltpu.make_async_copy(ob.at[me], orx.at[s], ors.at[s]).start()

                @pl.loop(1, n)
                def _(o):
                    d = lax.rem(me + o, n)
                    pltpu.make_async_remote_copy(
                        src_ref=ob.at[d], dst_ref=orx.at[s], send_sem=os, recv_sem=ors.at[s],
                        device_id=coords(d), device_id_type=MESH).start()

    for s in range(starts):
        pltpu.make_async_copy(orx.at[s], orx.at[s], ors.at[s]).wait()
        out_ref[:, s, :] = orx[s, 0:own_rows, 0:cols]
        w_ref[s : s + 1, :] = orx[s, own_rows : own_rows + 1, 0:cols]

    gram_rows("wait")
    mttkrp_rows("wait")
    for copy in c_copies + b_copies:
        copy.wait_send()

    @pl.when(is_solver)
    def _():
        rest = ob.at[pl.ds(0, n - 1)]
        pltpu.make_async_copy(rest, rest, os).wait()


def shards(sizes, tensor, factor_b, factor_c):
    na, nj, nk = sizes
    group = nj * nk
    n = na * group
    rows_i = tensor.shape[0]
    rows_b, starts, cols = factor_b.shape
    rows_c = factor_c.shape[0]
    own_rows = rows_i // group
    deep = -(-(own_rows + 1) // SUBS) * SUBS
    places = solver_places(sizes, starts)
    dma = pltpu.SemaphoreType.DMA
    f32 = jnp.float32
    vmem = pl.BlockSpec(memory_space=pltpu.VMEM)
    return pl.pallas_call(
        functools.partial(kernel, sizes, places, rows_i * na),
        out_shape=(
            jax.ShapeDtypeStruct((own_rows, starts, cols), f32),
            jax.ShapeDtypeStruct((starts, cols), f32),
        ),
        in_specs=[vmem] * 3,
        out_specs=(vmem, vmem),
        scratch_shapes=[
            pltpu.VMEM((nk, starts, rows_b, LANES), f32),
            pltpu.VMEM((nj, starts, rows_c, LANES), f32),
            pltpu.VMEM((group, rows_b, LANES), f32),
            pltpu.VMEM((group, rows_c, LANES), f32),
            pltpu.VMEM((starts, rows_i, LANES), f32),
            pltpu.VMEM((n, rows_i, LANES), f32),
            pltpu.VMEM((n, deep, LANES), f32),
            pltpu.VMEM((starts, deep, LANES), f32),
            dma((max(nk - 1, 1),)), dma((max(nk - 1, 1),)),
            dma((max(nj - 1, 1),)), dma((max(nj - 1, 1),)),
            dma((starts,)), dma, dma,
            dma((starts,)), dma,
            dma, dma((starts,)),
        ],
        compiler_params=pltpu.CompilerParams(collective_id=0, has_side_effects=True),
        name="factor_update",
    )(tensor, factor_b, factor_c)


def solution(mesh):
    sizes = (mesh.shape["ia"], mesh.shape["ja"], mesh.shape["ka"])
    in_specs = (P("ia", "ja", "ka"), P(("ja", "ka"), None, None), P(("ka", "ja"), None, None))
    out_specs = (P(("ia", "ja", "ka"), None, None), P())
    return jax.shard_map(functools.partial(shards, sizes), mesh=mesh, in_specs=in_specs,
                         out_specs=out_specs, check_vma=False)
```

```python
import functools

import jax
import jax.numpy as jnp
from jax import lax
from jax.experimental import pallas as pl
from jax.experimental.pallas import tpu as pltpu
from jax.sharding import PartitionSpec as P

MESH = pl.DeviceIdType.MESH
LANES = 128
SUBS = 8
HIGHEST = lax.Precision.HIGHEST


def solver_places(sizes, starts):
    na, nj, nk = sizes
    places = []
    for s in range(starts):
        ia = (s % 2) * (na // 2)
        ja = ((s // 2) * (nj // 2)) % nj
        ka = min(nk - 1, max(0, nk // 2 - 1 + (s // 2) % 2))
        places.append((ia, ja, ka))
    assert len(set(places)) == starts
    return places


def negative_inverse(tiles, cols):
    lane = lax.broadcasted_iota(jnp.int32, (SUBS, LANES), 1)
    sub = lax.broadcasted_iota(jnp.int32, (SUBS, LANES), 0)
    for k in range(0, cols, 2):
        v, p = k // SUBS, k % SUBS
        at0, at1 = lane == k, lane == k + 1
        both = at0 | at1
        row0 = jnp.broadcast_to(tiles[v][p : p + 1, :], (SUBS, LANES))
        row1 = jnp.broadcast_to(tiles[v][p + 1 : p + 2, :], (SUBS, LANES))
        col0 = [jnp.broadcast_to(t[:, k : k + 1], (SUBS, LANES)) for t in tiles]
        col1 = [jnp.broadcast_to(t[:, k + 1 : k + 2], (SUBS, LANES)) for t in tiles]
        a = jnp.broadcast_to(row0[:, k : k + 1], (SUBS, LANES))
        b = jnp.broadcast_to(row0[:, k + 1 : k + 2], (SUBS, LANES))
        d = jnp.broadcast_to(row1[:, k + 1 : k + 2], (SUBS, LANES))
        inv_a = 1.0 / a
        t = b * inv_a
        inv_s = 1.0 / (d - b * t)
        row0 = jnp.where(at0, -1.0, jnp.where(at1, 0.0, row0))
        row1 = jnp.where(at1, -1.0, jnp.where(at0, 0.0, row1))
        new1 = (row1 - t * row0) * inv_s
        new0 = row0 * inv_a - t * new1
        out = []
        for i, tile in enumerate(tiles):
            new = jnp.where(both, 0.0, tile) - col0[i] * new0 - col1[i] * new1
            if i == v:
                new = jnp.where(sub == p, new0, jnp.where(sub == p + 1, new1, new))
            out.append(new)
        tiles = out
    return tiles


def split(x):
    hi = x.astype(jnp.bfloat16)
    return hi, (x - hi.astype(jnp.float32)).astype(jnp.bfloat16)


def kernel(sizes, places, total_rows, own_rows, t_hbm, b_hbm, c_hbm, res,
           tv, bv, cv, bg, cg, bp, cp, gb, gc, mp, mr, ob, orx, inv,
           ts, ins, bs, br, cs, cr, gs, gbr, gcr, ms, mrs, os, ors):
    na, nj, nk = sizes
    group = nj * nk
    n = na * group
    starts, cols = bv.shape[1], bv.shape[2]
    rows_b = bv.shape[0]
    rows_i, rows_j, rows_k = tv.shape
    ia, ja, ka = (lax.axis_index("ia"), lax.axis_index("ja"), lax.axis_index("ka"))
    g = ja * nk + ka
    me = ia * group + g
    ids = [(pa * nj + pj) * nk + pk for pa, pj, pk in places]

    def coords(d):
        return (d // group, (d // nk) % nj, d % nk)

    barrier = pltpu.get_barrier_semaphore()

    def greet(target):
        pl.semaphore_signal(barrier, inc=1, device_id=target, device_id_type=MESH)

    for s in range(starts):
        @pl.when(me == ids[s])
        def _():
            @pl.loop(1, n)
            def _(o):
                greet(coords(lax.rem(me + o, n)))
    for o in range(1, nk):
        greet((ia, ja, lax.rem(ka + o, nk)))
    for o in range(1, nj):
        greet((ia, lax.rem(ja + o, nj), ka))

    load_b = pltpu.make_async_copy(b_hbm, bv, ins.at[0])
    load_c = pltpu.make_async_copy(c_hbm, cv, ins.at[1])
    load_t = pltpu.make_async_copy(t_hbm, tv, ts)
    load_b.start()
    load_c.start()
    load_t.start()

    bp[...] = jnp.zeros(bp.shape, jnp.float32)
    cp[...] = jnp.zeros(cp.shape, jnp.float32)
    mp[...] = jnp.zeros(mp.shape, jnp.float32)
    load_b.wait()
    for s in range(starts):
        rows = bv[:, s, :]
        bp[s, :, 0:cols] = rows
        bg[ka, :, s * cols : (s + 1) * cols] = rows
    load_c.wait()
    for s in range(starts):
        rows = cv[:, s, :]
        cp[s, :, 0:cols] = rows
        cg[ja, :, s * cols : (s + 1) * cols] = rows

    is_solver = functools.reduce(jnp.logical_or, [me == d for d in ids])
    near = (nk - 1) + (nj - 1)

    @pl.when(is_solver)
    def _():
        pl.semaphore_wait(barrier, near + starts - 1)

    @pl.when(jnp.logical_not(is_solver))
    def _():
        pl.semaphore_wait(barrier, near + starts)

    def push(src, dst, send, recv, place, target_id, act):
        @pl.when(me == target_id)
        def _():
            if act == "start":
                pltpu.make_async_copy(src, dst, recv).start()

        @pl.when(me != target_id)
        def _():
            copy = pltpu.make_async_remote_copy(
                src_ref=src, dst_ref=dst, send_sem=send, recv_sem=recv,
                device_id=place, device_id_type=MESH)
            if act == "start":
                copy.start()
            else:
                copy.wait_send()

    def gram_rows(act):
        for s, place in enumerate(places):
            @pl.when(ia == place[0])
            def _():
                push(bp.at[s], gb.at[g], gs.at[s], gbr, place, ids[s], act)

            @pl.when(ia == place[0] + 1)
            def _():
                push(cp.at[s], gc.at[g], gs.at[s], gcr, place, ids[s], act)

    gram_rows("start")
    c_copies = []
    for o in range(1, nj):
        c_copies.append(pltpu.make_async_remote_copy(
            src_ref=cg.at[ja], dst_ref=cg.at[ja], send_sem=cs.at[o - 1], recv_sem=cr.at[o - 1],
            device_id=(ia, lax.rem(ja + o, nj), ka), device_id_type=MESH))
    b_copies = []
    for o in range(1, nk):
        b_copies.append(pltpu.make_async_remote_copy(
            src_ref=bg.at[ka], dst_ref=bg.at[ka], send_sem=bs.at[o - 1], recv_sem=br.at[o - 1],
            device_id=(ia, ja, lax.rem(ka + o, nk)), device_id_type=MESH))
    for copy in c_copies + b_copies:
        copy.start()

    @pl.when(is_solver)
    def _():
        pltpu.make_async_copy(gb, gb, gbr).wait()
        pltpu.make_async_copy(gc, gc, gcr).wait()
        over_rows = (((0,), (0,)), ((), ()))
        rows_of_b = gb[...].reshape(gb.shape[0] * gb.shape[1], LANES)
        rows_of_c = gc[...].reshape(gc.shape[0] * gc.shape[1], LANES)
        gram_b = lax.dot_general(rows_of_b, rows_of_b, over_rows, precision=HIGHEST,
                                 preferred_element_type=jnp.float32)
        gram_c = lax.dot_general(rows_of_c, rows_of_c, over_rows, precision=HIGHEST,
                                 preferred_element_type=jnp.float32)
        normal = gram_b * gram_c
        tiles = [normal[i : i + SUBS, :] for i in range(0, cols, SUBS)]
        tiles = negative_inverse(tiles, cols)
        inv[0:cols, :] = jnp.concatenate(tiles, axis=0)
        inv[cols:LANES, :] = jnp.zeros((LANES - cols, LANES), jnp.float32)

    for o in range(1, nj):
        src = cg.at[lax.rem(ja - o + nj, nj)]
        pltpu.make_async_copy(src, src, cr.at[o - 1]).wait()
    load_t.wait()

    c_hi, c_lo = split(cg[...].reshape(rows_k, starts * cols))
    c_twice = jnp.concatenate([c_hi, c_hi], axis=0)
    acc = None
    for o in range(nk):
        q = lax.rem(ka - o + nk, nk)
        if o:
            src = bg.at[q]
            pltpu.make_async_copy(src, src, br.at[o - 1]).wait()
        at = pl.multiple_of(q * rows_b, rows_b)
        b_rows = bg[q]
        part = []
        for i in range(0, rows_i, SUBS):
            t_hi, t_lo = split(
                tv[i : i + SUBS, pl.ds(at, rows_b), :].reshape(SUBS * rows_b, rows_k))
            prod = jnp.dot(jnp.concatenate([t_hi, t_lo], axis=1), c_twice,
                           preferred_element_type=jnp.float32)
            prod = prod + jnp.dot(t_hi, c_lo, preferred_element_type=jnp.float32)
            part.append(jnp.sum(
                prod.reshape(SUBS, rows_b, starts * cols) * b_rows[None], axis=1))
        part = jnp.concatenate(part, axis=0)
        acc = part if acc is None else acc + part
    for s in range(starts):
        mp[s, :, 0:cols] = acc[:, s * cols : (s + 1) * cols]

    def mttkrp_rows(act):
        for s, place in enumerate(places):
            push(mp.at[s], mr.at[me], ms.at[s], mrs, place, ids[s], act)

    mttkrp_rows("start")

    @pl.when(is_solver)
    def _():
        pltpu.make_async_copy(mr, mr, mrs).wait()
        blocks = []
        for q in range(na):
            total = mr[q * group]
            for h in range(1, group):
                total = total + mr[q * group + h]
            blocks.append(total)
        mttkrp = jnp.concatenate(blocks, axis=0)
        raw = -jnp.dot(mttkrp, inv[...], precision=HIGHEST, preferred_element_type=jnp.float32)
        weight = jnp.sqrt(jnp.sum(raw * raw, axis=0, keepdims=True) / total_rows + 1e-06)
        final = raw / weight
        for d in range(n):
            ob[d, 0:own_rows, :] = final[d * own_rows : (d + 1) * own_rows, :]
            ob[d, own_rows : own_rows + 1, :] = weight

        for s in range(starts):
            @pl.when(me == ids[s])
            def _():
                pltpu.make_async_copy(ob.at[me], orx.at[s], ors.at[s]).start()

                @pl.loop(1, n)
                def _(o):
                    d = lax.rem(me + o, n)
                    pltpu.make_async_remote_copy(
                        src_ref=ob.at[d], dst_ref=orx.at[s], send_sem=os, recv_sem=ors.at[s],
                        device_id=coords(d), device_id_type=MESH).start()

    for s in range(starts):
        pltpu.make_async_copy(orx.at[s], orx.at[s], ors.at[s]).wait()
    res[...] = orx[...]

    gram_rows("wait")
    mttkrp_rows("wait")
    for copy in c_copies + b_copies:
        copy.wait_send()

    @pl.when(is_solver)
    def _():
        rest = ob.at[pl.ds(0, n - 1)]
        pltpu.make_async_copy(rest, rest, os).wait()


def place_kernel(res, out_ref, w_ref):
    own_rows, starts, cols = out_ref.shape
    for s in range(starts):
        out_ref[:, s, :] = res[s, 0:own_rows, 0:cols]
        w_ref[s : s + 1, :] = res[s, own_rows : own_rows + 1, 0:cols]


def shards(sizes, tensor, factor_b, factor_c):
    na, nj, nk = sizes
    group = nj * nk
    n = na * group
    rows_i = tensor.shape[0]
    rows_b, starts, cols = factor_b.shape
    rows_c = factor_c.shape[0]
    own_rows = rows_i // group
    deep = -(-(own_rows + 1) // SUBS) * SUBS
    places = solver_places(sizes, starts)
    dma = pltpu.SemaphoreType.DMA
    f32 = jnp.float32
    vmem = pl.BlockSpec(memory_space=pltpu.VMEM)
    res = pl.pallas_call(
        functools.partial(kernel, sizes, places, rows_i * na, own_rows),
        out_shape=jax.ShapeDtypeStruct((starts, deep, LANES), f32),
        in_specs=[pl.BlockSpec(memory_space=pl.ANY)] * 3,
        out_specs=vmem,
        scratch_shapes=[
            pltpu.VMEM(tensor.shape, f32),
            pltpu.VMEM(factor_b.shape, f32),
            pltpu.VMEM(factor_c.shape, f32),
            pltpu.VMEM((nk, rows_b, starts * cols), f32),
            pltpu.VMEM((nj, rows_c, starts * cols), f32),
            pltpu.VMEM((starts, rows_b, LANES), f32),
            pltpu.VMEM((starts, rows_c, LANES), f32),
            pltpu.VMEM((group, rows_b, LANES), f32),
            pltpu.VMEM((group, rows_c, LANES), f32),
            pltpu.VMEM((starts, rows_i, LANES), f32),
            pltpu.VMEM((n, rows_i, LANES), f32),
            pltpu.VMEM((n, deep, LANES), f32),
            pltpu.VMEM((starts, deep, LANES), f32),
            pltpu.VMEM((LANES, LANES), f32),
            dma, dma((2,)),
            dma((max(nk - 1, 1),)), dma((max(nk - 1, 1),)),
            dma((max(nj - 1, 1),)), dma((max(nj - 1, 1),)),
            dma((starts,)), dma, dma,
            dma((starts,)), dma,
            dma, dma((starts,)),
        ],
        compiler_params=pltpu.CompilerParams(collective_id=0, has_side_effects=True),
        name="factor_update",
    )(tensor, factor_b, factor_c)
    return pl.pallas_call(
        place_kernel,
        out_shape=(
            jax.ShapeDtypeStruct((own_rows, starts, cols), f32),
            jax.ShapeDtypeStruct((starts, cols), f32),
        ),
        in_specs=[vmem],
        out_specs=(vmem, vmem),
        name="place_rows",
    )(res)


def solution(mesh):
    sizes = (mesh.shape["ia"], mesh.shape["ja"], mesh.shape["ka"])
    in_specs = (P("ia", "ja", "ka"), P(("ja", "ka"), None, None), P(("ka", "ja"), None, None))
    out_specs = (P(("ia", "ja", "ka"), None, None), P())
    return jax.shard_map(functools.partial(shards, sizes), mesh=mesh, in_specs=in_specs,
                         out_specs=out_specs, check_vma=False)
```

```python
import functools

import jax
import jax.numpy as jnp
from jax import lax
from jax.experimental import pallas as pl
from jax.experimental.pallas import tpu as pltpu
from jax.sharding import PartitionSpec as P

MESH = pl.DeviceIdType.MESH
LANES = 128
SUBS = 8
UNROLLED = 64
HIGHEST = lax.Precision.HIGHEST


def solver_places(sizes, starts):
    na, nj, nk = sizes
    places = []
    for s in range(starts):
        ia = (s % 2) * (na // 2)
        ja = ((s // 2) * (nj // 2)) % nj
        ka = min(nk - 1, max(0, nk // 2 - 1 + (s // 2) % 2))
        places.append((ia, ja, ka))
    assert len(set(places)) == starts
    return places


def spread(row, k):
    return jnp.broadcast_to(row[:, k : k + 1], (SUBS, LANES))


def inverse_2x2(a, b, d):
    scale = 1.0 / (a * d - b * b)
    return d * scale, -b * scale, a * scale


def negative_inverse(tiles, cols):
    lane = lax.broadcasted_iota(jnp.int32, (SUBS, LANES), 1)
    sub = lax.broadcasted_iota(jnp.int32, (SUBS, LANES), 0)
    for k in range(0, cols, 4):
        v, p = k // SUBS, k % SUBS
        inside = (lane >= k) & (lane < k + 4)
        rows = [jnp.broadcast_to(tiles[v][p + m : p + m + 1, :], (SUBS, LANES)) for m in range(4)]
        e = {(m, q): spread(rows[m], k + q) for m in range(4) for q in range(m, 4)}
        cols_of = [[spread(t, k + m) for m in range(4)] for t in tiles]
        r0, r1, r2, r3 = [
            jnp.where(inside, jnp.where(lane == k + m, -1.0, 0.0), rows[m]) for m in range(4)]
        a00, a01, a11 = inverse_2x2(e[0, 0], e[0, 1], e[1, 1])
        w00 = a00 * e[0, 2] + a01 * e[1, 2]
        w01 = a00 * e[0, 3] + a01 * e[1, 3]
        w10 = a01 * e[0, 2] + a11 * e[1, 2]
        w11 = a01 * e[0, 3] + a11 * e[1, 3]
        s00, s01, s11 = inverse_2x2(
            e[2, 2] - (e[0, 2] * w00 + e[1, 2] * w10),
            e[2, 3] - (e[0, 2] * w01 + e[1, 2] * w11),
            e[3, 3] - (e[0, 3] * w01 + e[1, 3] * w11))
        y2 = r2 - (w00 * r0 + w10 * r1)
        y3 = r3 - (w01 * r0 + w11 * r1)
        x0 = a00 * r0 + a01 * r1
        x1 = a01 * r0 + a11 * r1
        z2 = s00 * y2 + s01 * y3
        z3 = s01 * y2 + s11 * y3
        z0 = x0 - (w00 * z2 + w01 * z3)
        z1 = x1 - (w10 * z2 + w11 * z3)
        out = []
        for i, tile in enumerate(tiles):
            c0, c1, c2, c3 = cols_of[i]
            new = (jnp.where(inside, 0.0, tile) - (c0 * z0 + c1 * z1)) - (c2 * z2 + c3 * z3)
            if i == v:
                for m, z in enumerate((z0, z1, z2, z3)):
                    new = jnp.where(sub == p + m, z, new)
            out.append(new)
        tiles = out
    return tiles


def unit_scales(normal, cols):
    at = [lax.broadcasted_iota(jnp.int32, normal.shape, a) for a in (0, 1)]
    marked = jnp.where(at[0] == at[1], jnp.where(at[0] < cols, normal, 1.0), 0.0)
    return (lax.rsqrt(jnp.sum(marked, axis=0, keepdims=True)),
            lax.rsqrt(jnp.sum(marked, axis=1, keepdims=True)))


def split(x):
    hi = x.astype(jnp.bfloat16)
    return hi, (x - hi.astype(jnp.float32)).astype(jnp.bfloat16)


def kernel(sizes, places, total_rows, own_rows, t_hbm, b_hbm, c_hbm, res,
           tv, bv, cv, bg, cg, bp, cp, gb, gc, mp, mr, ob, orx, inv,
           ts, ins, bs, br, cs, cr, gs, gbr, gcr, ms, mrs, os, ors):
    na, nj, nk = sizes
    group = nj * nk
    n = na * group
    starts, cols = bv.shape[1], bv.shape[2]
    rows_b = bv.shape[0]
    rows_i, rows_j, rows_k = tv.shape
    ia, ja, ka = (lax.axis_index("ia"), lax.axis_index("ja"), lax.axis_index("ka"))
    g = ja * nk + ka
    me = ia * group + g
    ids = [(pa * nj + pj) * nk + pk for pa, pj, pk in places]

    def coords(d):
        return (d // group, (d // nk) % nj, d % nk)

    barrier = pltpu.get_barrier_semaphore()

    def greet(target):
        pl.semaphore_signal(barrier, inc=1, device_id=target, device_id_type=MESH)

    for s in range(starts):
        @pl.when(me == ids[s])
        def _():
            @pl.loop(1, n)
            def _(o):
                greet(coords(lax.rem(me + o, n)))
    for o in range(1, nk):
        greet((ia, ja, lax.rem(ka + o, nk)))
    for o in range(1, nj):
        greet((ia, lax.rem(ja + o, nj), ka))

    load_b = pltpu.make_async_copy(b_hbm, bv, ins.at[0])
    load_c = pltpu.make_async_copy(c_hbm, cv, ins.at[1])
    load_t = pltpu.make_async_copy(t_hbm, tv, ts)
    load_b.start()
    load_c.start()
    load_t.start()

    bp[...] = jnp.zeros(bp.shape, jnp.float32)
    cp[...] = jnp.zeros(cp.shape, jnp.float32)
    mp[...] = jnp.zeros(mp.shape, jnp.float32)
    load_b.wait()
    for s in range(starts):
        rows = bv[:, s, :]
        bp[s, :, 0:cols] = rows
        bg[ka, :, s * cols : (s + 1) * cols] = rows
    load_c.wait()
    for s in range(starts):
        rows = cv[:, s, :]
        cp[s, :, 0:cols] = rows
        cg[ja, :, s * cols : (s + 1) * cols] = rows

    is_solver = functools.reduce(jnp.logical_or, [me == d for d in ids])
    near = (nk - 1) + (nj - 1)

    @pl.when(is_solver)
    def _():
        pl.semaphore_wait(barrier, near + starts - 1)

    @pl.when(jnp.logical_not(is_solver))
    def _():
        pl.semaphore_wait(barrier, near + starts)

    def push(src, dst, send, recv, place, target_id, act):
        @pl.when(me == target_id)
        def _():
            if act == "start":
                pltpu.make_async_copy(src, dst, recv).start()

        @pl.when(me != target_id)
        def _():
            copy = pltpu.make_async_remote_copy(
                src_ref=src, dst_ref=dst, send_sem=send, recv_sem=recv,
                device_id=place, device_id_type=MESH)
            if act == "start":
                copy.start()
            else:
                copy.wait_send()

    def gram_rows(act):
        for s, place in enumerate(places):
            @pl.when(ia == place[0])
            def _():
                push(bp.at[s], gb.at[g], gs.at[s], gbr, place, ids[s], act)

            @pl.when(ia == place[0] + 1)
            def _():
                push(cp.at[s], gc.at[g], gs.at[s], gcr, place, ids[s], act)

    gram_rows("start")
    c_copies = []
    for o in range(1, nj):
        c_copies.append(pltpu.make_async_remote_copy(
            src_ref=cg.at[ja], dst_ref=cg.at[ja], send_sem=cs.at[o - 1], recv_sem=cr.at[o - 1],
            device_id=(ia, lax.rem(ja + o, nj), ka), device_id_type=MESH))
    b_copies = []
    for o in range(1, nk):
        b_copies.append(pltpu.make_async_remote_copy(
            src_ref=bg.at[ka], dst_ref=bg.at[ka], send_sem=bs.at[o - 1], recv_sem=br.at[o - 1],
            device_id=(ia, ja, lax.rem(ka + o, nk)), device_id_type=MESH))
    for copy in c_copies + b_copies:
        copy.start()

    @pl.when(is_solver)
    def _():
        pltpu.make_async_copy(gb, gb, gbr).wait()
        pltpu.make_async_copy(gc, gc, gcr).wait()
        over_rows = (((0,), (0,)), ((), ()))
        rows_of_b = gb[...].reshape(gb.shape[0] * gb.shape[1], LANES)
        rows_of_c = gc[...].reshape(gc.shape[0] * gc.shape[1], LANES)
        gram_b = lax.dot_general(rows_of_b, rows_of_b, over_rows, precision=HIGHEST,
                                 preferred_element_type=jnp.float32)
        gram_c = lax.dot_general(rows_of_c, rows_of_c, over_rows, precision=HIGHEST,
                                 preferred_element_type=jnp.float32)
        normal = gram_b * gram_c
        scale_row, scale_col = unit_scales(normal, cols)
        normal = normal * scale_row * scale_col
        tiles = [normal[i : i + SUBS, :] for i in range(0, cols, SUBS)]
        tiles = negative_inverse(tiles, cols)
        inv[0:cols, :] = jnp.concatenate(tiles, axis=0) * scale_row * scale_col[0:cols]
        inv[cols:LANES, :] = jnp.zeros((LANES - cols, LANES), jnp.float32)

    for o in range(1, nj):
        src = cg.at[lax.rem(ja - o + nj, nj)]
        pltpu.make_async_copy(src, src, cr.at[o - 1]).wait()
    load_t.wait()

    c_hi, c_lo = split(cg[...].reshape(rows_k, starts * cols))
    c_twice = jnp.concatenate([c_hi, c_hi], axis=0)
    acc = None
    for o in range(nk):
        q = lax.rem(ka - o + nk, nk)
        if o:
            src = bg.at[q]
            pltpu.make_async_copy(src, src, br.at[o - 1]).wait()
        at = pl.multiple_of(q * rows_b, rows_b)
        b_rows = bg[q]
        part = []
        for i in range(0, rows_i, SUBS):
            t_hi, t_lo = split(
                tv[i : i + SUBS, pl.ds(at, rows_b), :].reshape(SUBS * rows_b, rows_k))
            prod = jnp.dot(jnp.concatenate([t_hi, t_lo], axis=1), c_twice,
                           preferred_element_type=jnp.float32)
            prod = prod + jnp.dot(t_hi, c_lo, preferred_element_type=jnp.float32)
            part.append(jnp.sum(
                prod.reshape(SUBS, rows_b, starts * cols) * b_rows[None], axis=1))
        part = jnp.concatenate(part, axis=0)
        acc = part if acc is None else acc + part
    for s in range(starts):
        mp[s, :, 0:cols] = acc[:, s * cols : (s + 1) * cols]

    def mttkrp_rows(act):
        for s, place in enumerate(places):
            push(mp.at[s], mr.at[me], ms.at[s], mrs, place, ids[s], act)

    mttkrp_rows("start")

    @pl.when(is_solver)
    def _():
        pltpu.make_async_copy(mr, mr, mrs).wait()
        blocks = []
        for q in range(na):
            total = mr[q * group]
            for h in range(1, group):
                total = total + mr[q * group + h]
            blocks.append(total)
        mttkrp = jnp.concatenate(blocks, axis=0)
        raw = -jnp.dot(mttkrp, inv[...], precision=HIGHEST, preferred_element_type=jnp.float32)
        weight = jnp.sqrt(jnp.sum(raw * raw, axis=0, keepdims=True) / total_rows + 1e-06)
        final = raw / weight
        for d in range(n):
            ob[d, 0:own_rows, :] = final[d * own_rows : (d + 1) * own_rows, :]
            ob[d, own_rows : own_rows + 1, :] = weight

        for s in range(starts):
            @pl.when(me == ids[s])
            def _():
                pltpu.make_async_copy(ob.at[me], orx.at[s], ors.at[s]).start()

                def send(d):
                    pltpu.make_async_remote_copy(
                        src_ref=ob.at[d], dst_ref=orx.at[s], send_sem=os, recv_sem=ors.at[s],
                        device_id=coords(d), device_id_type=MESH).start()

                if n <= UNROLLED:
                    for d in range(n - 1, -1, -1):
                        if d != ids[s]:
                            send(d)
                else:
                    @pl.loop(1, n)
                    def _(o):
                        send(lax.rem(me + o, n))

    for s in range(starts):
        pltpu.make_async_copy(orx.at[s], orx.at[s], ors.at[s]).wait()
    res[...] = orx[...]

    gram_rows("wait")
    mttkrp_rows("wait")
    for copy in c_copies + b_copies:
        copy.wait_send()

    @pl.when(is_solver)
    def _():
        rest = ob.at[pl.ds(0, n - 1)]
        pltpu.make_async_copy(rest, rest, os).wait()


def place_kernel(res, out_ref, w_ref):
    own_rows, starts, cols = out_ref.shape
    for s in range(starts):
        out_ref[:, s, :] = res[s, 0:own_rows, 0:cols]
        w_ref[s : s + 1, :] = res[s, own_rows : own_rows + 1, 0:cols]


def shards(sizes, tensor, factor_b, factor_c):
    na, nj, nk = sizes
    group = nj * nk
    n = na * group
    rows_i = tensor.shape[0]
    rows_b, starts, cols = factor_b.shape
    rows_c = factor_c.shape[0]
    own_rows = rows_i // group
    deep = -(-(own_rows + 1) // SUBS) * SUBS
    places = solver_places(sizes, starts)
    dma = pltpu.SemaphoreType.DMA
    f32 = jnp.float32
    vmem = pl.BlockSpec(memory_space=pltpu.VMEM)
    res = pl.pallas_call(
        functools.partial(kernel, sizes, places, rows_i * na, own_rows),
        out_shape=jax.ShapeDtypeStruct((starts, deep, LANES), f32),
        in_specs=[pl.BlockSpec(memory_space=pl.ANY)] * 3,
        out_specs=vmem,
        scratch_shapes=[
            pltpu.VMEM(tensor.shape, f32),
            pltpu.VMEM(factor_b.shape, f32),
            pltpu.VMEM(factor_c.shape, f32),
            pltpu.VMEM((nk, rows_b, starts * cols), f32),
            pltpu.VMEM((nj, rows_c, starts * cols), f32),
            pltpu.VMEM((starts, rows_b, LANES), f32),
            pltpu.VMEM((starts, rows_c, LANES), f32),
            pltpu.VMEM((group, rows_b, LANES), f32),
            pltpu.VMEM((group, rows_c, LANES), f32),
            pltpu.VMEM((starts, rows_i, LANES), f32),
            pltpu.VMEM((n, rows_i, LANES), f32),
            pltpu.VMEM((n, deep, LANES), f32),
            pltpu.VMEM((starts, deep, LANES), f32),
            pltpu.VMEM((LANES, LANES), f32),
            dma, dma((2,)),
            dma((max(nk - 1, 1),)), dma((max(nk - 1, 1),)),
            dma((max(nj - 1, 1),)), dma((max(nj - 1, 1),)),
            dma((starts,)), dma, dma,
            dma((starts,)), dma,
            dma, dma((starts,)),
        ],
        compiler_params=pltpu.CompilerParams(collective_id=0, has_side_effects=True),
        name="factor_update",
    )(tensor, factor_b, factor_c)
    return pl.pallas_call(
        place_kernel,
        out_shape=(
            jax.ShapeDtypeStruct((own_rows, starts, cols), f32),
            jax.ShapeDtypeStruct((starts, cols), f32),
        ),
        in_specs=[vmem],
        out_specs=(vmem, vmem),
        name="place_rows",
    )(res)


def solution(mesh):
    sizes = (mesh.shape["ia"], mesh.shape["ja"], mesh.shape["ka"])
    in_specs = (P("ia", "ja", "ka"), P(("ja", "ka"), None, None), P(("ka", "ja"), None, None))
    out_specs = (P(("ia", "ja", "ka"), None, None), P())
    return jax.shard_map(functools.partial(shards, sizes), mesh=mesh, in_specs=in_specs,
                         out_specs=out_specs, check_vma=False)
```

```python
import functools

import jax
import jax.numpy as jnp
from jax import lax
from jax.experimental import pallas as pl
from jax.experimental.pallas import tpu as pltpu
from jax.sharding import PartitionSpec as P

MESH = pl.DeviceIdType.MESH
LANES = 128
SUBS = 8
UNROLLED = 64
HIGHEST = lax.Precision.HIGHEST


def solver_places(sizes, starts):
    na, nj, nk = sizes
    places = []
    for s in range(starts):
        ia = (s % 2) * (na // 2)
        ja = ((s // 2) * (nj // 2)) % nj
        ka = min(nk - 1, max(0, nk // 2 - 1 + (s // 2) % 2))
        places.append((ia, ja, ka))
    assert len(set(places)) == starts
    return places


def spread(row, k):
    return jnp.broadcast_to(row[:, k : k + 1], (SUBS, LANES))


def inverse_2x2(a, b, d):
    scale = 1.0 / (a * d - b * b)
    return d * scale, -b * scale, a * scale


def negative_inverse(tiles, first, last):
    lane = lax.broadcasted_iota(jnp.int32, (SUBS, LANES), 1)
    sub = lax.broadcasted_iota(jnp.int32, (SUBS, LANES), 0)
    for k in range(first, last, 4):
        v, p = k // SUBS, k % SUBS
        inside = (lane >= k) & (lane < k + 4)
        rows = [jnp.broadcast_to(tiles[v][p + m : p + m + 1, :], (SUBS, LANES)) for m in range(4)]
        e = {(m, q): spread(rows[m], k + q) for m in range(4) for q in range(m, 4)}
        cols_of = [[spread(t, k + m) for m in range(4)] for t in tiles]
        r0, r1, r2, r3 = [
            jnp.where(inside, jnp.where(lane == k + m, -1.0, 0.0), rows[m]) for m in range(4)]
        a00, a01, a11 = inverse_2x2(e[0, 0], e[0, 1], e[1, 1])
        w00 = a00 * e[0, 2] + a01 * e[1, 2]
        w01 = a00 * e[0, 3] + a01 * e[1, 3]
        w10 = a01 * e[0, 2] + a11 * e[1, 2]
        w11 = a01 * e[0, 3] + a11 * e[1, 3]
        s00, s01, s11 = inverse_2x2(
            e[2, 2] - (e[0, 2] * w00 + e[1, 2] * w10),
            e[2, 3] - (e[0, 2] * w01 + e[1, 2] * w11),
            e[3, 3] - (e[0, 3] * w01 + e[1, 3] * w11))
        y2 = r2 - (w00 * r0 + w10 * r1)
        y3 = r3 - (w01 * r0 + w11 * r1)
        x0 = a00 * r0 + a01 * r1
        x1 = a01 * r0 + a11 * r1
        z2 = s00 * y2 + s01 * y3
        z3 = s01 * y2 + s11 * y3
        z0 = x0 - (w00 * z2 + w01 * z3)
        z1 = x1 - (w10 * z2 + w11 * z3)
        out = []
        for i, tile in enumerate(tiles):
            c0, c1, c2, c3 = cols_of[i]
            new = (jnp.where(inside, 0.0, tile) - (c0 * z0 + c1 * z1)) - (c2 * z2 + c3 * z3)
            if i == v:
                for m, z in enumerate((z0, z1, z2, z3)):
                    new = jnp.where(sub == p + m, z, new)
            out.append(new)
        tiles = out
    return tiles


def unit_scales(normal, cols):
    at = [lax.broadcasted_iota(jnp.int32, normal.shape, a) for a in (0, 1)]
    marked = jnp.where(at[0] == at[1], jnp.where(at[0] < cols, normal, 1.0), 0.0)
    return (lax.rsqrt(jnp.sum(marked, axis=0, keepdims=True)),
            lax.rsqrt(jnp.sum(marked, axis=1, keepdims=True)))


def split(x):
    hi = x.astype(jnp.bfloat16)
    return hi, (x - hi.astype(jnp.float32)).astype(jnp.bfloat16)


def kernel(sizes, places, total_rows, own_rows, t_hbm, b_hbm, c_hbm, res,
           tv, bv, cv, bg, cg, bp, cp, gb, gc, mp, mr, ob, orx, inv, scales,
           ts, ins, bs, br, cs, cr, gs, gbr, gcr, ms, mrs, os, ors):
    na, nj, nk = sizes
    group = nj * nk
    n = na * group
    starts, cols = bv.shape[1], bv.shape[2]
    rows_b = bv.shape[0]
    rows_i, rows_j, rows_k = tv.shape
    ia, ja, ka = (lax.axis_index("ia"), lax.axis_index("ja"), lax.axis_index("ka"))
    g = ja * nk + ka
    me = ia * group + g
    ids = [(pa * nj + pj) * nk + pk for pa, pj, pk in places]

    def coords(d):
        return (d // group, (d // nk) % nj, d % nk)

    barrier = pltpu.get_barrier_semaphore()

    def greet(target):
        pl.semaphore_signal(barrier, inc=1, device_id=target, device_id_type=MESH)

    for s in range(starts):
        @pl.when(me == ids[s])
        def _():
            @pl.loop(1, n)
            def _(o):
                greet(coords(lax.rem(me + o, n)))
    for o in range(1, nk):
        greet((ia, ja, lax.rem(ka + o, nk)))
    for o in range(1, nj):
        greet((ia, lax.rem(ja + o, nj), ka))

    load_b = pltpu.make_async_copy(b_hbm, bv, ins.at[0])
    load_c = pltpu.make_async_copy(c_hbm, cv, ins.at[1])
    load_t = pltpu.make_async_copy(t_hbm, tv, ts)
    load_b.start()
    load_c.start()
    load_t.start()

    bp[...] = jnp.zeros(bp.shape, jnp.float32)
    cp[...] = jnp.zeros(cp.shape, jnp.float32)
    mp[...] = jnp.zeros(mp.shape, jnp.float32)
    load_b.wait()
    for s in range(starts):
        rows = bv[:, s, :]
        bp[s, :, 0:cols] = rows
        bg[ka, :, s * cols : (s + 1) * cols] = rows
    load_c.wait()
    for s in range(starts):
        rows = cv[:, s, :]
        cp[s, :, 0:cols] = rows
        cg[ja, :, s * cols : (s + 1) * cols] = rows

    is_solver = functools.reduce(jnp.logical_or, [me == d for d in ids])
    near = (nk - 1) + (nj - 1)
    early = cols // 2 // SUBS * SUBS

    @pl.when(is_solver)
    def _():
        pl.semaphore_wait(barrier, near + starts - 1)

    @pl.when(jnp.logical_not(is_solver))
    def _():
        pl.semaphore_wait(barrier, near + starts)

    def push(src, dst, send, recv, place, target_id, act):
        @pl.when(me == target_id)
        def _():
            if act == "start":
                pltpu.make_async_copy(src, dst, recv).start()

        @pl.when(me != target_id)
        def _():
            copy = pltpu.make_async_remote_copy(
                src_ref=src, dst_ref=dst, send_sem=send, recv_sem=recv,
                device_id=place, device_id_type=MESH)
            if act == "start":
                copy.start()
            else:
                copy.wait_send()

    def gram_rows(act):
        for s, place in enumerate(places):
            @pl.when(ia == place[0])
            def _():
                push(bp.at[s], gb.at[g], gs.at[s], gbr, place, ids[s], act)

            @pl.when(ia == place[0] + 1)
            def _():
                push(cp.at[s], gc.at[g], gs.at[s], gcr, place, ids[s], act)

    gram_rows("start")
    c_copies = []
    for o in range(1, nj):
        c_copies.append(pltpu.make_async_remote_copy(
            src_ref=cg.at[ja], dst_ref=cg.at[ja], send_sem=cs.at[o - 1], recv_sem=cr.at[o - 1],
            device_id=(ia, lax.rem(ja + o, nj), ka), device_id_type=MESH))
    b_copies = []
    for o in range(1, nk):
        b_copies.append(pltpu.make_async_remote_copy(
            src_ref=bg.at[ka], dst_ref=bg.at[ka], send_sem=bs.at[o - 1], recv_sem=br.at[o - 1],
            device_id=(ia, ja, lax.rem(ka + o, nk)), device_id_type=MESH))
    for copy in c_copies + b_copies:
        copy.start()

    @pl.when(is_solver)
    def _():
        pltpu.make_async_copy(gb, gb, gbr).wait()
        pltpu.make_async_copy(gc, gc, gcr).wait()
        over_rows = (((0,), (0,)), ((), ()))
        rows_of_b = gb[...].reshape(gb.shape[0] * gb.shape[1], LANES)
        rows_of_c = gc[...].reshape(gc.shape[0] * gc.shape[1], LANES)
        gram_b = lax.dot_general(rows_of_b, rows_of_b, over_rows, precision=HIGHEST,
                                 preferred_element_type=jnp.float32)
        gram_c = lax.dot_general(rows_of_c, rows_of_c, over_rows, precision=HIGHEST,
                                 preferred_element_type=jnp.float32)
        normal = gram_b * gram_c
        scale_row, scale_col = unit_scales(normal, cols)
        normal = normal * scale_row * scale_col
        tiles = [normal[i : i + SUBS, :] for i in range(0, cols, SUBS)]
        tiles = negative_inverse(tiles, 0, early)
        inv[0:cols, :] = jnp.concatenate(tiles, axis=0)
        scales[0] = jnp.broadcast_to(scale_row, scales.shape[1:])
        scales[1] = jnp.broadcast_to(scale_col, scales.shape[1:])
        inv[cols:LANES, :] = jnp.zeros((LANES - cols, LANES), jnp.float32)

    for o in range(1, nj):
        src = cg.at[lax.rem(ja - o + nj, nj)]
        pltpu.make_async_copy(src, src, cr.at[o - 1]).wait()
    load_t.wait()

    c_hi, c_lo = split(cg[...].reshape(rows_k, starts * cols))
    c_twice = jnp.concatenate([c_hi, c_hi], axis=0)
    acc = None
    for o in range(nk):
        q = lax.rem(ka - o + nk, nk)
        if o:
            src = bg.at[q]
            pltpu.make_async_copy(src, src, br.at[o - 1]).wait()
        at = pl.multiple_of(q * rows_b, rows_b)
        b_rows = bg[q]
        part = []
        for i in range(0, rows_i, SUBS):
            t_hi, t_lo = split(
                tv[i : i + SUBS, pl.ds(at, rows_b), :].reshape(SUBS * rows_b, rows_k))
            prod = jnp.dot(jnp.concatenate([t_hi, t_lo], axis=1), c_twice,
                           preferred_element_type=jnp.float32)
            prod = prod + jnp.dot(t_hi, c_lo, preferred_element_type=jnp.float32)
            part.append(jnp.sum(
                prod.reshape(SUBS, rows_b, starts * cols) * b_rows[None], axis=1))
        part = jnp.concatenate(part, axis=0)
        acc = part if acc is None else acc + part
    for s in range(starts):
        mp[s, :, 0:cols] = acc[:, s * cols : (s + 1) * cols]

    def mttkrp_rows(act):
        for s, place in enumerate(places):
            push(mp.at[s], mr.at[me], ms.at[s], mrs, place, ids[s], act)

    mttkrp_rows("start")

    @pl.when(is_solver)
    def _():
        tiles = [inv[i : i + SUBS, :] for i in range(0, cols, SUBS)]
        tiles = negative_inverse(tiles, early, cols)
        inv[0:cols, :] = jnp.concatenate(tiles, axis=0) * scales[0, 0:cols] * scales[1, 0:cols]
        pltpu.make_async_copy(mr, mr, mrs).wait()
        blocks = []
        for q in range(na):
            total = mr[q * group]
            for h in range(1, group):
                total = total + mr[q * group + h]
            blocks.append(total)
        mttkrp = jnp.concatenate(blocks, axis=0)
        raw = -jnp.dot(mttkrp, inv[...], precision=HIGHEST, preferred_element_type=jnp.float32)
        weight = jnp.sqrt(jnp.sum(raw * raw, axis=0, keepdims=True) / total_rows + 1e-06)
        final = raw / weight
        for d in range(n):
            ob[d, 0:own_rows, :] = final[d * own_rows : (d + 1) * own_rows, :]
            ob[d, own_rows : own_rows + 1, :] = weight

        for s in range(starts):
            @pl.when(me == ids[s])
            def _():
                pltpu.make_async_copy(ob.at[me], orx.at[s], ors.at[s]).start()

                def send(d):
                    pltpu.make_async_remote_copy(
                        src_ref=ob.at[d], dst_ref=orx.at[s], send_sem=os, recv_sem=ors.at[s],
                        device_id=coords(d), device_id_type=MESH).start()

                if n <= UNROLLED:
                    for d in sorted(range(n), key=lambda d: sum(coords(d))):
                        if d != ids[s]:
                            send(d)
                else:
                    @pl.loop(1, n)
                    def _(o):
                        send(lax.rem(me + o, n))

    for s in range(starts):
        pltpu.make_async_copy(orx.at[s], orx.at[s], ors.at[s]).wait()
    res[...] = orx[...]

    gram_rows("wait")
    mttkrp_rows("wait")
    for copy in c_copies + b_copies:
        copy.wait_send()

    @pl.when(is_solver)
    def _():
        rest = ob.at[pl.ds(0, n - 1)]
        pltpu.make_async_copy(rest, rest, os).wait()


def place_kernel(res, out_ref, w_ref):
    own_rows, starts, cols = out_ref.shape
    for s in range(starts):
        out_ref[:, s, :] = res[s, 0:own_rows, 0:cols]
        w_ref[s : s + 1, :] = res[s, own_rows : own_rows + 1, 0:cols]


def shards(sizes, tensor, factor_b, factor_c):
    na, nj, nk = sizes
    group = nj * nk
    n = na * group
    rows_i = tensor.shape[0]
    rows_b, starts, cols = factor_b.shape
    rows_c = factor_c.shape[0]
    own_rows = rows_i // group
    deep = -(-(own_rows + 1) // SUBS) * SUBS
    places = solver_places(sizes, starts)
    dma = pltpu.SemaphoreType.DMA
    f32 = jnp.float32
    vmem = pl.BlockSpec(memory_space=pltpu.VMEM)
    res = pl.pallas_call(
        functools.partial(kernel, sizes, places, rows_i * na, own_rows),
        out_shape=jax.ShapeDtypeStruct((starts, deep, LANES), f32),
        in_specs=[pl.BlockSpec(memory_space=pl.ANY)] * 3,
        out_specs=vmem,
        scratch_shapes=[
            pltpu.VMEM(tensor.shape, f32),
            pltpu.VMEM(factor_b.shape, f32),
            pltpu.VMEM(factor_c.shape, f32),
            pltpu.VMEM((nk, rows_b, starts * cols), f32),
            pltpu.VMEM((nj, rows_c, starts * cols), f32),
            pltpu.VMEM((starts, rows_b, LANES), f32),
            pltpu.VMEM((starts, rows_c, LANES), f32),
            pltpu.VMEM((group, rows_b, LANES), f32),
            pltpu.VMEM((group, rows_c, LANES), f32),
            pltpu.VMEM((starts, rows_i, LANES), f32),
            pltpu.VMEM((n, rows_i, LANES), f32),
            pltpu.VMEM((n, deep, LANES), f32),
            pltpu.VMEM((starts, deep, LANES), f32),
            pltpu.VMEM((LANES, LANES), f32),
            pltpu.VMEM((2, LANES, LANES), f32),
            dma, dma((2,)),
            dma((max(nk - 1, 1),)), dma((max(nk - 1, 1),)),
            dma((max(nj - 1, 1),)), dma((max(nj - 1, 1),)),
            dma((starts,)), dma, dma,
            dma((starts,)), dma,
            dma, dma((starts,)),
        ],
        compiler_params=pltpu.CompilerParams(collective_id=0, has_side_effects=True),
        name="factor_update",
    )(tensor, factor_b, factor_c)
    return pl.pallas_call(
        place_kernel,
        out_shape=(
            jax.ShapeDtypeStruct((own_rows, starts, cols), f32),
            jax.ShapeDtypeStruct((starts, cols), f32),
        ),
        in_specs=[vmem],
        out_specs=(vmem, vmem),
        name="place_rows",
    )(res)


def solution(mesh):
    sizes = (mesh.shape["ia"], mesh.shape["ja"], mesh.shape["ka"])
    in_specs = (P("ia", "ja", "ka"), P(("ja", "ka"), None, None), P(("ka", "ja"), None, None))
    out_specs = (P(("ia", "ja", "ka"), None, None), P())
    return jax.shard_map(functools.partial(shards, sizes), mesh=mesh, in_specs=in_specs,
                         out_specs=out_specs, check_vma=False)
```
